256 devices in a mesh: member: 32 (over z_hi, x, y), row: 8 (over z_lo, core).
Axes of the slice: x: 4, y: 4, z: 8 (z_hi: 2, z_lo: 4; z = z_hi * 4 + z_lo), core: 2. Of those that a mesh axis runs over, the one named last changes fastest.
Arguments:
- fields: float32 [64, 3, 128, 1024], P('member', None, 'row'), may hold values from -1.5 to 1.5
- bathymetry: int32 [128, 1024], P('row'), may hold values from 250 to 300
- copy_lists: int32 [3, 6, 64], replicated, may hold values from 0 to 63, as said below
Outputs:
- final_fields: float32 [64, 3, 128, 1024], P('member', None, 'row')
The draws below stay inside these ranges and needn't reach their ends.
Inputs may be any that keep to these rules, and one draw needn't show every extreme that they name: copy_lists[c, s, m] is m or m xor 2 to the power s; members m and m xor 2 to the power s either both keep their own state or both take the same one of the two.
All inputs are finite; a program needn't handle non-finite values.
Results may differ from the reference program's by a relative error of at most 0.00002.
Values sent between devices are 32-bit elements; how exact they have to be, the bound alone decides.
No kernel may reach another device: no remote copies, remote signals or barrier semaphores. Data moves between devices by JAX's collectives and lax.ppermute only.
A program may use at most 64 MiB of HBM per device.

```python
import jax
import jax.numpy as jnp

NX = 1024
STEPS = 4
CYCLES = 3
NY = 128
MEMBERS = 64
SECTIONS = 6


def draw_copy_lists(key, part):
    outcome = jax.random.randint(key, (CYCLES, SECTIONS, MEMBERS), 0, 3).astype(jnp.int32)
    members = jnp.arange(MEMBERS, dtype=jnp.int32)
    powers = (2 ** jnp.arange(SECTIONS, dtype=jnp.int32))[None, :, None]
    partner = jnp.bitwise_xor(members[None, None, :], powers)
    lower = jnp.minimum(members[None, None, :], partner)
    upper = jnp.maximum(members[None, None, :], partner)
    lower_full = jnp.broadcast_to(lower, (CYCLES, SECTIONS, MEMBERS)).astype(jnp.int32)
    pair_kind = jnp.take_along_axis(outcome, lower_full, axis=2)
    keep = jnp.broadcast_to(members[None, None, :], (CYCLES, SECTIONS, MEMBERS))
    sources = jnp.where(pair_kind == 0, keep, jnp.where(pair_kind == 1, lower_full, upper))
    return sources.astype(jnp.int32)


def with_ends(result, key, low, high):
    shape = result.shape
    place = [jax.random.randint(jax.random.fold_in(key, axis), (), 0, shape[axis]) for axis in range(len(shape))]
    result = result.at[tuple(place)].set(low)
    longest = shape.index(max(shape))
    place[longest] = (place[longest] + 1) % shape[longest]
    return result.at[tuple(place)].set(high)


def steps_of(key, shape, cuts, smallest, high):
    def one(position, parts):
        draws = jax.random.uniform(jax.random.fold_in(jax.random.fold_in(key, 6), position), (parts,), jnp.float32, smallest / len(cuts), high / len(cuts))
        return jnp.repeat(jnp.exp(draws), shape[position] // parts).reshape((-1,) + (1,) * (len(shape) - position - 1))

    loudness = one(*cuts[0])
    for cut in cuts[1:]:
        loudness = loudness * one(*cut)
    return loudness


def centred(stream_key, shape, width, limit, pieces=(), kind=jnp.bfloat16):
    result = width * jax.random.normal(stream_key, shape, jnp.float32)
    if pieces:
        result = result * steps_of(stream_key, shape, pieces, -0.22, 0.18)
    return jnp.clip(result, -limit, limit).astype(kind)


def setup_inputs(seed: int = 0) -> dict:
    keys = jax.random.split(jax.random.key(seed), 4)
    return {
        "fields": centred(keys[0], (MEMBERS, 3, NY, NX), 0.3, 1.5, ((0, 32), (2, 8)), jnp.float32),
        "bathymetry": with_ends(jax.random.randint(keys[1], (NY, NX), 250, 301), jax.random.fold_in(keys[1], 1), 250, 300).astype(jnp.int32),
        "copy_lists": draw_copy_lists(jax.random.fold_in(keys[3], 71), 0),
    }


gravity = 2.0
coriolis = 0.1
friction = 0.02
time_step = 0.25


def rates(padded, depth_pad):
    height = padded[:, 0]
    east = padded[:, 1]
    north = padded[:, 2]
    column = depth_pad + height
    flux_x = column * east
    flux_y = column * north
    diff_x = (jnp.roll(flux_x, -1, -1) - jnp.roll(flux_x, 1, -1))[:, 1:-1]
    diff_y = flux_y[:, 2:] - flux_y[:, :-2]
    rate_h = -0.5 * (diff_x + diff_y)
    slope_x = (jnp.roll(height, -1, -1) - jnp.roll(height, 1, -1))[:, 1:-1]
    slope_y = height[:, 2:] - height[:, :-2]
    east_mid = east[:, 1:-1]
    north_mid = north[:, 1:-1]
    rate_u = -0.5 * gravity * slope_x + coriolis * north_mid - friction * east_mid
    rate_v = -0.5 * gravity * slope_y - coriolis * east_mid - friction * north_mid
    return jnp.stack([rate_h, rate_u, rate_v], 1)


def wrap_rows(field):
    return jnp.concatenate([field[..., -1:, :], field, field[..., :1, :]], axis=-2)


def reference(fields, bathymetry, copy_lists):
    depth = bathymetry.astype(jnp.float32) / 100.0
    depth_pad = wrap_rows(depth)
    current = fields
    for cycle_no in range(CYCLES):
        for step_no in range(STEPS):
            first_rate = rates(wrap_rows(current), depth_pad)
            middle = current + time_step * first_rate
            second_rate = rates(wrap_rows(middle), depth_pad)
            current = current + (0.5 * time_step) * (first_rate + second_rate)
        for section_no in range(SECTIONS):
            current = jnp.take(current, copy_lists[cycle_no, section_no], axis=0)
    return current
```

```python
import functools

import jax
import jax.numpy as jnp
from jax import lax
from jax.experimental import pallas as pl
from jax.experimental.pallas import tpu as pltpu
from jax.sharding import PartitionSpec as P

STEPS = 4
CYCLES = 3
HALO = 2 * STEPS
LANES = 128
WINDOW = 64

gravity = 2.0
coriolis = 0.1
friction = 0.02
time_step = 0.25


def turn(x, shift, axis):
    return pltpu.roll(x, shift % x.shape[axis], axis)


def advance(h, u, v, depth, scale):
    column = depth + h
    flux_x = column * u
    flux_y = column * v
    diff_x = turn(flux_x, -1, 1) - turn(flux_x, 1, 1)
    diff_y = turn(flux_y, -1, 0) - turn(flux_y, 1, 0)
    slope_x = turn(h, -1, 1) - turn(h, 1, 1)
    slope_y = turn(h, -1, 0) - turn(h, 1, 0)
    add_h = (-0.5 * scale) * (diff_x + diff_y)
    add_u = (scale * coriolis) * v - (0.5 * scale * gravity) * slope_x
    add_v = (-scale * coriolis) * u - (0.5 * scale * gravity) * slope_y
    return add_h, add_u, add_v


def one_step(h, u, v, depth):
    keep = 1.0 - time_step * friction
    dh, du, dv = advance(h, u, v, depth, time_step)
    mh, mu, mv = h + dh, keep * u + du, keep * v + dv
    half = 0.5 * time_step
    keep = 0.5 - half * friction
    dh, du, dv = advance(mh, mu, mv, depth, half)
    return 0.5 * (h + mh) + dh, 0.5 * u + (keep * mu + du), 0.5 * v + (keep * mv + dv)


def source_of(lists, cycle, sections, members, m):
    for section in range(sections - 1, -1, -1):
        m = lists[(cycle * sections + section) * members + m]
    return m


def first_kernel(place, fields, depth, up, down, packed, depth_window, state, depth_full):
    count, parts, rows, width = fields.shape
    depth_full[0:HALO] = up[count * parts]
    depth_full[HALO : HALO + rows] = depth[...]
    depth_full[HALO + rows :] = down[count * parts]
    for m in range(count):
        for f in range(parts):
            state[m, f, 0:HALO] = up[m * parts + f]
            state[m, f, HALO : HALO + rows] = fields[m, f]
            state[m, f, HALO + rows :] = down[m * parts + f]

    def step(i, carry):
        m = i // STEPS
        h, u, v = one_step(state[m, 0], state[m, 1], state[m, 2], depth_full[...])
        state[m, 0] = h
        state[m, 1] = u
        state[m, 2] = v
        return carry

    lax.fori_loop(0, count * STEPS, step, 0)

    margin = (WINDOW - width // packed.shape[0]) // 2
    stride = width // packed.shape[0]
    ways = LANES // stride
    lane = lax.broadcasted_iota(jnp.int32, (rows, width), 1) % LANES
    for f in range(parts):
        first = state[0, f, HALO : HALO + rows]
        second = state[1, f, HALO : HALO + rows]
        for j in range(ways):
            both = jnp.where(
                lane < WINDOW,
                turn(first, margin - stride * j, 1),
                turn(second, margin - stride * j + WINDOW, 1),
            )
            for k in range(width // LANES):
                packed[ways * k + j, f] = both[:, LANES * k : LANES * (k + 1)]

    start = place[0] * stride
    shift = lax.rem(width + margin - start, width)
    window = pltpu.roll(depth_full[...], shift, 1)[:, :LANES]
    lane = lax.broadcasted_iota(jnp.int32, window.shape, 1)
    depth_window[...] = jnp.where(lane < WINDOW, window, turn(window, WINDOW, 1))


def gathered(lists, cycle, sections, members, pair, blocks):
    loads = []
    for half in range(2):
        source = source_of(lists, cycle, sections, members, 2 * pair + half)
        shift = WINDOW * ((source + half) % 2)
        loads.append([pltpu.roll(x, shift, 1) for x in blocks(source // 2)])
    lane = lax.broadcasted_iota(jnp.int32, loads[0][0].shape, 1)
    return [jnp.where(lane < WINDOW, a, b) for a, b in zip(*loads)]


def cycle_of(lists, cycle, sections, members, pair, blocks, depth):
    h, u, v = gathered(lists, cycle, sections, members, pair, blocks)
    for _ in range(STEPS):
        h, u, v = one_step(h, u, v, depth)
    return h, u, v


def middle_kernel(sections, members, lists, own, up, down, depth, top, bottom):
    def blocks(pair):
        return [jnp.concatenate([up[pair, f], own[pair, f], down[pair, f]], 0) for f in range(3)]

    def one(pair, carry):
        result = cycle_of(lists, 0, sections, members, pair, blocks, depth[...])
        for f in range(3):
            top[pair, f] = result[f][HALO : 2 * HALO]
            bottom[pair, f] = result[f][2 * HALO : 3 * HALO]
        return carry

    lax.fori_loop(0, members // 2, one, 0, unroll=2)


def last_kernel(sections, members, stride, lists, own_top, own_bottom, up, down, depth, packed, state):
    def blocks(pair):
        return [
            jnp.concatenate([up[pair, f], own_top[pair, f], own_bottom[pair, f], down[pair, f]], 0)
            for f in range(3)
        ]

    def one(pair, carry):
        result = cycle_of(lists, 1, sections, members, pair, blocks, depth[...])
        for f in range(3):
            state[pair, f] = result[f][HALO : 3 * HALO]
        return carry

    lax.fori_loop(0, members // 2, one, 0, unroll=2)

    margin = (WINDOW - stride) // 2
    group = lax.broadcasted_iota(jnp.int32, (HALO, LANES), 1) // stride

    def pack(pair, carry):
        sources = [source_of(lists, 2, sections, members, 2 * pair + half) for half in range(2)]
        for f in range(3):
            total = None
            for tile in range(2):
                for half in range(2):
                    source = sources[half]
                    place = 2 * tile + half
                    shift = (stride * place - margin) % LANES + WINDOW * (source % 2)
                    piece = pltpu.roll(state[source // 2, f, HALO * tile : HALO * (tile + 1)], lax.rem(shift, LANES), 1)
                    total = piece if total is None else jnp.where(group == place, piece, total)
            packed[pair, f] = total
        return carry

    lax.fori_loop(0, members // 2, pack, 0, unroll=2)


def unpack_kernel(stride, arrived, out):
    ways = LANES // stride
    group = lax.broadcasted_iota(jnp.int32, (HALO, LANES), 1) // stride
    for f in range(3):
        for k in range(arrived.shape[0] // ways):
            pieces = [arrived[ways * k + j, f] for j in range(ways)]
            for tile in range(2):
                for half in range(2):
                    place = 2 * tile + half
                    total = None
                    for j in range(ways):
                        piece = turn(pieces[j], stride * (j - place), 1)
                        total = piece if total is None else jnp.where(group == j, piece, total)
                    out[half, f, HALO * tile : HALO * (tile + 1), LANES * k : LANES * (k + 1)] = total


def body(fields, bathymetry, copy_lists):
    count, parts, rows, width = fields.shape
    devices = lax.axis_size("member")
    members = count * devices
    sections = copy_lists.shape[1]
    stride = width // devices
    ring = lax.axis_size("row")
    up_route = [(i, (i + 1) % ring) for i in range(ring)]
    down_route = [(j, i) for i, j in up_route]
    vmem = pl.BlockSpec(memory_space=pltpu.VMEM)
    smem = pl.BlockSpec(memory_space=pltpu.SMEM)
    f32 = functools.partial(jax.ShapeDtypeStruct, dtype=jnp.float32)

    depth = bathymetry.astype(jnp.float32) / 100.0
    place = lax.axis_index("member").astype(jnp.int32).reshape(1)
    lists = copy_lists.reshape(-1)
    planes = fields.reshape(count * parts, rows, width)
    top = jnp.concatenate([planes[:, :HALO], depth[None, :HALO]], 0)
    bottom = jnp.concatenate([planes[:, rows - HALO :], depth[None, rows - HALO :]], 0)
    up = lax.ppermute(bottom, "row", up_route)
    down = lax.ppermute(top, "row", down_route)
    packed, depth_window = pl.pallas_call(
        first_kernel,
        out_shape=(f32((devices, parts, rows, LANES)), f32((rows + 2 * HALO, LANES))),
        in_specs=[smem] + [vmem] * 4,
        out_specs=(vmem, vmem),
        scratch_shapes=[
            pltpu.VMEM((count, parts, rows + 2 * HALO, width), jnp.float32),
            pltpu.VMEM((rows + 2 * HALO, width), jnp.float32),
        ],
        name="first",
    )(place, fields, depth, up, down)
    own = lax.all_to_all(packed, "member", 0, 0, tiled=True)

    up = lax.ppermute(own[:, :, rows - HALO :], "row", up_route)
    down = lax.ppermute(own[:, :, :HALO], "row", down_route)
    edge = f32((devices, parts, HALO, LANES))
    top, bottom = pl.pallas_call(
        functools.partial(middle_kernel, sections, members),
        out_shape=(edge, edge),
        in_specs=[smem] + [vmem] * 4,
        out_specs=(vmem, vmem),
        name="middle",
    )(lists, own, up, down, depth_window)

    up = lax.ppermute(bottom, "row", up_route)
    down = lax.ppermute(top, "row", down_route)
    packed = pl.pallas_call(
        functools.partial(last_kernel, sections, members, stride),
        out_shape=edge,
        in_specs=[smem] + [vmem] * 5,
        out_specs=vmem,
        scratch_shapes=[pltpu.VMEM((devices, parts, rows, LANES), jnp.float32)],
        name="last",
    )(lists, top, bottom, up, down, depth_window)
    arrived = lax.all_to_all(packed, "member", 0, 0, tiled=True)
    return pl.pallas_call(
        functools.partial(unpack_kernel, stride),
        out_shape=f32(fields.shape),
        in_specs=[vmem],
        out_specs=vmem,
        name="unpack",
    )(arrived)


def solution(mesh):
    placed = (P("member", None, "row", None), P("row", None), P())
    return jax.shard_map(
        body, mesh=mesh, in_specs=placed, out_specs=P("member", None, "row", None), check_vma=False
    )
```

```python
import functools

import jax
import jax.numpy as jnp
from jax import lax
from jax.experimental import pallas as pl
from jax.experimental.pallas import tpu as pltpu
from jax.sharding import PartitionSpec as P

STEPS = 4
HALO = 2 * STEPS
LANES = 128
SUBLANES = 8
HEIGHT_UNIT = 2.0**-5
SPEED_UNIT = 2.0**-3

gravity = 2.0
coriolis = 0.1
friction = 0.02
time_step = 0.25


def turn(x, shift, axis):
    return pltpu.roll(x, shift % x.shape[axis], axis)


def euler(h, u, v, depth, joined):
    keep = 1.0 - time_step * friction
    cross = time_step * coriolis
    column = each(lambda a, b: a + b, depth, h)
    flux_x = each(lambda a, b: a * b, column, u)
    flux_y = each(lambda a, b: a * b, column, v)
    next_h = each(lambda a, b, c: a - (b + c), h, along(flux_x, joined), across(flux_y))
    next_u = each(lambda a, b, c: (keep * a + cross * b) - c, u, v, along(h, joined))
    next_v = each(lambda a, b, c: (keep * b - cross * a) - c, u, v, across(h))
    return next_h, next_u, next_v


def each(f, *grids):
    return [[f(*values) for values in zip(*rows)] for rows in zip(*grids)]


def across(x):
    above = [[turn(y, 1, 0) for y in x[-1]]] + x[:-1]
    below = x[1:] + [[turn(y, -1, 0) for y in x[0]]]
    return each(lambda a, b: b - a, above, below)


def along(x, joined):
    left = each(lambda y: turn(y, 1, 1), x)
    right = each(lambda y: turn(y, -1, 1), x)
    if joined:
        lane = lax.broadcasted_iota(jnp.int32, x[0][0].shape, 1)
        left = [[jnp.where(lane == 0, a, b) for a, b in zip([y[-1]] + y[:-1], y)] for y in left]
        right = [[jnp.where(lane == LANES - 1, a, b) for a, b in zip(y[1:] + [y[0]], y)] for y in right]
    return each(lambda a, b: b - a, left, right)


def one_step(state, depth, joined):
    ahead = euler(*euler(*state, depth, joined), depth, joined)
    return [each(lambda a, b: 0.5 * (a + b), x, y) for x, y in zip(state, ahead)]


def source_of(lists, cycles, sections, members, m):
    for section in range(cycles * sections - 1, -1, -1):
        m = lists[section * members + m]
    return m


def edge_kernel(fields, bathymetry, top, bottom):
    count, parts, rows, width = fields.shape
    for m in range(count):
        for f in range(parts):
            unit = HEIGHT_UNIT if f == 0 else SPEED_UNIT
            top[m * parts + f] = unit * fields[m, f, 0:HALO]
            bottom[m * parts + f] = unit * fields[m, f, rows - HALO : rows]
    depth = scaled_depth(bathymetry[...])
    top[count * parts] = depth[0:HALO]
    bottom[count * parts] = depth[rows - HALO :]


def scaled_depth(hundredths):
    return hundredths.astype(jnp.float32) * (0.01 * HEIGHT_UNIT)


def spread(ref, *index):
    ways = ref.shape[-2] // SUBLANES
    return [ref[(*index, pl.ds(q, SUBLANES, stride=ways), slice(None))] for q in range(ways)]


def unspread(ref, values, *index):
    for q, value in enumerate(values):
        ref[(*index, pl.ds(q, SUBLANES, stride=len(values)), slice(None))] = value


def take_cycle(depth, state):
    count, parts, blocks = state.shape[:3]

    def grid(ref, *index):
        return [list(x) for x in zip(*[spread(ref, *index, k) for k in range(blocks)])]

    def step(i, carry):
        m = i // STEPS
        result = one_step([grid(state, m, f) for f in range(parts)], grid(depth), True)
        for f in range(parts):
            for k in range(blocks):
                unspread(state, [x[k] for x in result[f]], m, f, k)
        return carry

    lax.fori_loop(0, count * STEPS, step, 0)


def fill(state, up, top, bottom, down):
    count, parts, blocks = state.shape[:3]
    for m in range(count):
        for f in range(parts):
            for i, piece in enumerate((up, top, bottom, down)):
                rows = piece(m, f)
                for k in range(blocks):
                    state[m, f, k, HALO * i : HALO * (i + 1)] = rows[:, LANES * k : LANES * (k + 1)]


def put_edges(state, top, bottom):
    count, parts, blocks = state.shape[:3]
    for m in range(count):
        for f in range(parts):
            for k in range(blocks):
                for i, ref in enumerate((top, bottom)):
                    piece = state[m, f, k, HALO * (i + 1) : HALO * (i + 2)]
                    ref[m * parts + f, :, LANES * k : LANES * (k + 1)] = piece


def plane(ref):
    return lambda m, f: ref[3 * m + f]


def first_kernel(fields, bathymetry, up, down, top, bottom, depth, state):
    count, parts, rows, width = fields.shape
    own = scaled_depth(bathymetry[...])
    pieces = (up[count * parts], own[:HALO], own[HALO:], down[count * parts])
    for i, piece in enumerate(pieces):
        for k in range(width // LANES):
            depth[k, HALO * i : HALO * (i + 1)] = piece[:, LANES * k : LANES * (k + 1)]

    def part(first):
        def rows_of(m, f):
            return (HEIGHT_UNIT if f == 0 else SPEED_UNIT) * fields[m, f, first : first + HALO]

        return rows_of

    fill(state, plane(up), part(0), part(HALO), plane(down))
    take_cycle(depth, state)
    put_edges(state, top, bottom)


def middle_kernel(depth, up, own_top, own_bottom, down, top, bottom, state):
    fill(state, plane(up), plane(own_top), plane(own_bottom), plane(down))
    take_cycle(depth, state)
    put_edges(state, top, bottom)


def last_kernel(depth, up, own_top, own_bottom, down, packed, state):
    fill(state, plane(up), plane(own_top), plane(own_bottom), plane(down))
    take_cycle(depth, state)
    count, parts, blocks = state.shape[:3]
    ways = packed.shape[0] // blocks
    stride = LANES // ways
    group = lax.broadcasted_iota(jnp.int32, (HALO, LANES), 1) // stride
    for f in range(parts):
        for k in range(blocks):
            pieces = [state[m, f, k, HALO * (t + 1) : HALO * (t + 2)] for t in range(2) for m in range(count)]
            for j in range(ways):
                total = None
                for i, piece in enumerate(pieces):
                    moved = turn(piece, stride * (i - j), 1)
                    total = moved if total is None else jnp.where(group == i, moved, total)
                packed[ways * k + j, f] = total


def gather_kernel(cycles, sections, members, stride, lists, before, after):
    parts = before.shape[1]
    member = lax.broadcasted_iota(jnp.int32, before.shape[2:], 1) // stride & 1

    def one(pair, carry):
        halves = []
        for half in range(2):
            source = source_of(lists, cycles, sections, members, 2 * pair + half)
            shift = (stride * (half - (source & 1))) & (LANES - 1)
            halves.append([pltpu.roll(before[source >> 1, f], shift, 1) for f in range(parts)])
        for f in range(parts):
            after[pair, f] = jnp.where(member == 0, halves[0][f], halves[1][f])
        return carry

    lax.fori_loop(0, members // 2, one, 0, unroll=4)


def unpack_kernel(stride, arrived, out):
    ways = LANES // stride
    group = lax.broadcasted_iota(jnp.int32, (HALO, LANES), 1) // stride
    for f in range(3):
        unit = 1 / (HEIGHT_UNIT if f == 0 else SPEED_UNIT)
        for k in range(arrived.shape[0] // ways):
            pieces = [unit * arrived[ways * k + j, f] for j in range(ways)]
            for tile in range(2):
                for half in range(2):
                    place = 2 * tile + half
                    total = None
                    for j in range(ways):
                        piece = turn(pieces[j], stride * (j - place), 1)
                        total = piece if total is None else jnp.where(group == j, piece, total)
                    out[half, f, HALO * tile : HALO * (tile + 1), LANES * k : LANES * (k + 1)] = total


def body(fields, bathymetry, copy_lists):
    count, parts, rows, width = fields.shape
    devices = lax.axis_size("member")
    members = count * devices
    cycles, sections = copy_lists.shape[:2]
    ring = lax.axis_size("row")
    up_route = [(i, (i + 1) % ring) for i in range(ring)]
    down_route = [(j, i) for i, j in up_route]
    vmem = pl.BlockSpec(memory_space=pltpu.VMEM)
    smem = pl.BlockSpec(memory_space=pltpu.SMEM)
    f32 = functools.partial(jax.ShapeDtypeStruct, dtype=jnp.float32)
    tall = rows + 2 * HALO
    state = pltpu.VMEM((count, parts, width // LANES, tall, LANES), jnp.float32)
    columns = f32((devices, parts, HALO, LANES))

    def call(kernel, out_shape, *args, scratch=(), scalars=0, name=None):
        many = isinstance(out_shape, tuple)
        return pl.pallas_call(
            kernel,
            out_shape=out_shape,
            in_specs=[smem] * scalars + [vmem] * (len(args) - scalars),
            out_specs=(vmem,) * len(out_shape) if many else vmem,
            scratch_shapes=scratch,
            compiler_params=pltpu.CompilerParams(vmem_limit_bytes=16 << 20),
            name=name,
        )(*args)

    def exchange(top, bottom):
        return lax.ppermute(bottom, "row", up_route), lax.ppermute(top, "row", down_route)

    line = f32((count * parts + 1, HALO, width))
    up, down = exchange(*call(edge_kernel, (line, line), fields, bathymetry, name="edge"))
    line = f32((count * parts, HALO, width))
    top, bottom, depth = call(
        first_kernel,
        (line, line, f32((width // LANES, tall, LANES))),
        fields,
        bathymetry,
        up,
        down,
        scratch=[state],
        name="first",
    )
    for _ in range(cycles - 2):
        up, down = exchange(top, bottom)
        top, bottom = call(
            middle_kernel, (line, line), depth, up, top, bottom, down, scratch=[state], name="middle"
        )
    up, down = exchange(top, bottom)
    packed = call(last_kernel, columns, depth, up, top, bottom, down, scratch=[state], name="last")

    own = lax.all_to_all(packed, "member", 0, 0, tiled=True)
    chosen = call(
        functools.partial(gather_kernel, cycles, sections, members, width // devices),
        columns,
        copy_lists.reshape(-1),
        own,
        scalars=1,
        name="gather",
    )
    arrived = lax.all_to_all(chosen, "member", 0, 0, tiled=True)
    return call(
        functools.partial(unpack_kernel, width // devices), f32(fields.shape), arrived, name="unpack"
    )


def solution(mesh):
    placed = (P("member", None, "row", None), P("row", None), P())
    return jax.shard_map(
        body, mesh=mesh, in_specs=placed, out_specs=P("member", None, "row", None), check_vma=False
    )
```

```python
import functools

import jax
import jax.numpy as jnp
from jax import lax
from jax.experimental import pallas as pl
from jax.experimental.pallas import tpu as pltpu
from jax.sharding import PartitionSpec as P

STEPS = 4
HALO = 2 * STEPS
LANES = 128
SUBLANES = 8
HEIGHT_UNIT = 2.0**-5
SPEED_UNIT = 2.0**-3

gravity = 2.0
coriolis = 0.1
friction = 0.02
time_step = 0.25


def turn(x, shift, axis):
    return pltpu.roll(x, shift % x.shape[axis], axis)


def euler(h, u, v, depth):
    keep = 1.0 - time_step * friction
    cross = time_step * coriolis
    column = each(lambda a, b: a + b, depth, h)
    flux_x = each(lambda a, b: a * b, column, u)
    flux_y = each(lambda a, b: a * b, column, v)
    next_h = each(lambda a, b, c: a - (b + c), h, along(flux_x), across(flux_y))
    next_u = each(lambda a, b, c: (keep * a + cross * b) - c, u, v, along(h))
    next_v = each(lambda a, b, c: (keep * b - cross * a) - c, u, v, across(h))
    return next_h, next_u, next_v


def each(f, *grids):
    return [[f(*values) for values in zip(*rows)] for rows in zip(*grids)]


def across(x):
    above = [[turn(y, 1, 0) for y in x[-1]]] + x[:-1]
    below = x[1:] + [[turn(y, -1, 0) for y in x[0]]]
    return each(lambda a, b: b - a, above, below)


def along(x):
    return [[b - a for a, b in zip([turn(y[-1], 1, 1)] + y[:-1], y[1:] + [turn(y[0], -1, 1)])] for y in x]


def one_step(state, depth):
    ahead = euler(*euler(*state, depth), depth)
    return [each(lambda a, b: 0.5 * (a + b), x, y) for x, y in zip(state, ahead)]


def swap_groups(x):
    x, width = list(x), LANES // len(x)
    group = lax.broadcasted_iota(jnp.int32, x[0].shape, 1) // width
    bit = 1
    while bit < len(x):
        low = group & bit == 0
        for i in range(len(x)):
            if not i & bit:
                a, b = x[i], x[i + bit]
                x[i] = jnp.where(low, a, turn(b, width * bit, 1))
                x[i + bit] = jnp.where(low, turn(a, -width * bit, 1), b)
        bit *= 2
    return x


def pick(x, index):
    return jnp.take_along_axis(x, index, axis=1)


def interleave(x):
    ways = len(x)
    lane = lax.broadcasted_iota(jnp.int32, x[0].shape, 1)
    width = LANES // ways
    return swap_groups([pick(y, ways * (lane % width) + lane // width) for y in x])


def blocks_of(x):
    return [x[:, LANES * k : LANES * (k + 1)] for k in range(x.shape[1] // LANES)]


def offsets(odd):
    return [pl.multiple_of(HALO * x, HALO) for x in (3 * odd, 1 + odd, 2 - odd, 3 - 3 * odd)]


def edge_kernel(odd, fields, bathymetry, *refs):
    count, parts, rows, width = fields.shape
    outs, (held, held_depth, sems) = refs[: 2 * count], refs[2 * count :]
    copies = [pltpu.make_async_copy(bathymetry, held_depth, sems.at[count])]
    copies += [pltpu.make_async_copy(fields.at[m], held.at[m], sems.at[m]) for m in range(count)]
    for copy in copies:
        copy.start()
    _, outer, inner, _ = offsets(odd[0])
    copies[0].wait()
    depth = []
    for first in (outer, inner):
        depth.append(interleave(blocks_of(scaled_depth(held_depth[pl.ds(first - HALO, HALO)]))))
    for m in range(count):
        copies[1 + m].wait()
        for i, first in enumerate((outer, inner)):
            write_blocks(outs[2 * m + i], parts, depth[(i + m) % 2])
            for f in range(parts):
                unit = HEIGHT_UNIT if f == 0 else SPEED_UNIT
                write_blocks(outs[2 * m + i], f, interleave(blocks_of(unit * held[m, f, pl.ds(first - HALO, HALO)])))


def write_blocks(ref, index, values):
    for k, value in enumerate(values):
        ref[index, :, LANES * k : LANES * (k + 1)] = value


def scaled_depth(hundredths):
    return hundredths.astype(jnp.float32) * (0.01 * HEIGHT_UNIT)


def spread(ref, *index):
    ways = ref.shape[-2] // SUBLANES
    return [ref[(*index, pl.ds(q, SUBLANES, stride=ways), slice(None))] for q in range(ways)]


def unspread(ref, values, *index):
    for q, value in enumerate(values):
        ref[(*index, pl.ds(q, SUBLANES, stride=len(values)), slice(None))] = value


def take_steps(depth, state, steps):
    parts, blocks = state.shape[:2]

    def grid(ref, *index):
        return [list(x) for x in zip(*[spread(ref, *index, k) for k in range(blocks)])]

    def step(i, carry):
        result = one_step([grid(state, f) for f in range(parts)], grid(depth))
        for f in range(parts):
            for k in range(blocks):
                unspread(state, [x[k] for x in result[f]], f, k)
        return carry

    lax.fori_loop(0, steps, step, 0)


def fill(place, blocks, pieces):
    for first, piece in pieces:
        for k in range(blocks):
            place(k, pl.ds(first, piece.shape[0]))[...] = piece[:, LANES * k : LANES * (k + 1)]


def plane(ref, f):
    return lambda k, rows: ref.at[f, k, rows]


def first_round(odd, depth, state, tile, pieces):
    parts, blocks = state.shape[:2]
    places = offsets(odd[0])
    for f in range(parts):
        fill(plane(state, f), blocks, [(first, ref[f]) for first, ref in zip(places, pieces)])
    take_steps(depth, state, STEPS)
    for f in range(parts):
        write_blocks(tile, f, [state[f, k, HALO : 3 * HALO] for k in range(blocks)])


def first_kernel(odd, beyond, own_outer, own_inner, beside, tile, depth, state):
    pieces = beyond, own_outer, own_inner, beside
    places = offsets(odd[0])
    parts, blocks = state.shape[:2]
    fill(lambda k, rows: depth.at[k, rows], blocks, [(first, ref[parts]) for first, ref in zip(places, pieces)])
    first_round(odd, depth, state, tile, pieces)


def second_kernel(odd, depth, beyond, own_outer, own_inner, beside, tile, tall_depth, state):
    parts, blocks = state.shape[:2]
    far = pl.multiple_of(5 * HALO * odd[0], HALO)
    near = pl.multiple_of(5 * HALO * (1 - odd[0]), HALO)
    fill(lambda k, rows: tall_depth.at[k, rows], blocks, [(far, beyond[parts]), (near, beside[parts])])
    tall_depth[:, HALO : 5 * HALO] = depth[...]
    first_round(odd, depth, state, tile, (beyond, own_outer, own_inner, beside))


def second_round(odd, depth, state, beyond, own, beside, steps):
    rows = own.shape[1]
    far = pl.multiple_of(2 * rows * odd[0], rows)
    near = pl.multiple_of(2 * rows * (1 - odd[0]), rows)
    for f in range(own.shape[0]):
        fill(plane(state, f), state.shape[1], [(far, beyond[f]), (rows, own[f]), (near, beside[f])])
    take_steps(depth, state, steps)


def third_kernel(steps, odd, depth, beyond, own, beside, tile, state):
    second_round(odd, depth, state, beyond, own, beside, steps)
    parts, blocks = state.shape[:2]
    for f in range(parts):
        write_blocks(tile, f, [state[f, k, 2 * HALO : 4 * HALO] for k in range(blocks)])


def last_kernel(steps, odd, depth, beyond, own, beside, other, packed, state):
    second_round(odd, depth, state, beyond, own, beside, steps)
    parts, blocks = state.shape[:2]
    ways = packed.shape[0] // blocks
    for f in range(parts):
        for k in range(blocks):
            columns = slice(LANES * k, LANES * (k + 1))
            pieces = []
            for i in range(2):
                pieces.append(other[f, HALO * i : HALO * (i + 1), columns])
                pieces.append(state[f, k, HALO * (i + 2) : HALO * (i + 3)])
            for j, value in enumerate(swap_groups(pieces)):
                packed[ways * k + j, f] = value


def source_kernel(lists, sources):
    members = sources.shape[0]

    def one(member, carry):
        source = member
        for section in range(lists.shape[0] // members - 1, -1, -1):
            source = lists[section * members + source]
        sources[member] = source
        return carry

    lax.fori_loop(0, members, one, 0, unroll=16)


def gather_kernel(stride, sources, before, after):
    pairs, parts = before.shape[:2]
    member = lax.broadcasted_iota(jnp.int32, before.shape[2:], 1) // stride & 1

    def one(pair, carry):
        halves = []
        for half in range(2):
            source = sources[2 * pair + half]
            shift = (stride * (half - (source & 1))) & (LANES - 1)
            halves.append([pltpu.roll(before[source >> 1, f], shift, 1) for f in range(parts)])
        for f in range(parts):
            after[pair, f] = jnp.where(member == 0, halves[0][f], halves[1][f])
        return carry

    lax.fori_loop(0, pairs, one, 0, unroll=8)


def unpack_kernel(arrived, out):
    count, parts, rows, width = out.shape
    blocks = width // LANES
    ways = arrived.shape[0] // blocks
    lane = lax.broadcasted_iota(jnp.int32, (HALO, LANES), 1)
    order = LANES // blocks * (lane % blocks) + lane // blocks
    for f in range(parts):
        unit = 1 / (HEIGHT_UNIT if f == 0 else SPEED_UNIT)
        for j in range(ways):
            pieces = swap_groups([unit * arrived[ways * k + j, f] for k in range(blocks)])
            for i, piece in enumerate(pieces):
                half, m, low = i // 4, i // 2 % 2, i % 2
                k = 2 * j + low
                out[m, f, HALO * half : HALO * (half + 1), LANES * k : LANES * (k + 1)] = pick(piece, order)


def body(fields, bathymetry, copy_lists):
    count, parts, rows, width = fields.shape
    devices = lax.axis_size("member")
    cycles = copy_lists.shape[0]
    ring = lax.axis_size("row")
    within = [(i, i ^ 1) for i in range(ring)]
    across_chips = [(i, (i + 1 if i % 2 else i - 1) % ring) for i in range(ring)]
    odd = (lax.axis_index("row") % 2).astype(jnp.int32).reshape(1)
    vmem = pl.BlockSpec(memory_space=pltpu.VMEM)
    smem = pl.BlockSpec(memory_space=pltpu.SMEM)
    f32 = functools.partial(jax.ShapeDtypeStruct, dtype=jnp.float32)
    columns = f32((devices, parts, HALO, LANES))

    def call(kernel, out_shape, *args, scratch=(), scalars=1, space=vmem, grant=16, name=None):
        many = isinstance(out_shape, tuple)
        return pl.pallas_call(
            kernel,
            out_shape=out_shape,
            in_specs=[smem] * scalars + [space] * (len(args) - scalars),
            out_specs=(vmem,) * len(out_shape) if many else vmem,
            scratch_shapes=scratch,
            compiler_params=pltpu.CompilerParams(vmem_limit_bytes=grant << 20),
            name=name,
        )(*args)

    def exchange(outer, inner):
        return lax.ppermute(outer, "row", across_chips), lax.ppermute(inner, "row", within)

    blocks = width // LANES
    half = f32((parts + 1, HALO, width))
    tile = f32((parts, rows, width))
    edges = call(
        edge_kernel,
        (half,) * (2 * count),
        odd,
        fields,
        bathymetry,
        scratch=[
            pltpu.VMEM(fields.shape, fields.dtype),
            pltpu.VMEM(bathymetry.shape, bathymetry.dtype),
            pltpu.SemaphoreType.DMA((count + 1,)),
        ],
        space=pl.BlockSpec(memory_space=pltpu.HBM),
        name="edge",
    )
    now = [edges[2 * m : 2 * m + 2] for m in range(count)]
    around = [exchange(*x) for x in now]
    pieces = [(beyond, *x, beside) for x, (beyond, beside) in zip(now, around)]

    def state(tall):
        return [pltpu.VMEM((parts, blocks, tall, LANES), jnp.float32)]

    tall = rows + 2 * HALO
    first, depth = call(
        first_kernel, (tile, f32((blocks, tall, LANES))), odd, *pieces[0], scratch=state(tall), name="first"
    )
    around = [exchange(first, first)]
    tall = rows * 3
    second, tall_depth = call(
        second_kernel,
        (tile, f32((blocks, tall, LANES))),
        odd,
        depth,
        *pieces[1],
        scratch=state(rows + 2 * HALO),
        name="second",
    )
    around.append(exchange(second, second))
    steps = (cycles - 1) * STEPS
    first = call(
        functools.partial(third_kernel, steps),
        tile,
        odd,
        tall_depth,
        around[0][0],
        first,
        around[0][1],
        scratch=state(tall),
        name="third",
    )
    packed = call(
        functools.partial(last_kernel, steps),
        columns,
        odd,
        tall_depth,
        around[1][0],
        second,
        around[1][1],
        first,
        scratch=state(tall),
        name="last",
    )

    own = lax.all_to_all(packed, "member", 0, 0, tiled=True)
    sources = pl.pallas_call(
        source_kernel,
        out_shape=jax.ShapeDtypeStruct((count * devices,), jnp.int32),
        in_specs=[smem],
        out_specs=smem,
        name="sources",
    )(copy_lists.reshape(-1))
    chosen = call(
        functools.partial(gather_kernel, width // devices), columns, sources, own, name="gather"
    )
    arrived = lax.all_to_all(chosen, "member", 0, 0, tiled=True)
    return call(unpack_kernel, f32(fields.shape), arrived, scalars=0, name="unpack")


def solution(mesh):
    placed = (P("member", None, "row", None), P("row", None), P())
    return jax.shard_map(
        body, mesh=mesh, in_specs=placed, out_specs=P("member", None, "row", None), check_vma=False
    )
```

```python
import functools

import jax
import jax.numpy as jnp
from jax import lax
from jax.experimental import pallas as pl
from jax.experimental.pallas import tpu as pltpu
from jax.sharding import PartitionSpec as P

STEPS = 4
HALO = 2 * STEPS
LANES = 128
SUBLANES = 8
HEIGHT_UNIT = 2.0**-5
SPEED_UNIT = 2.0**-3

gravity = 2.0
coriolis = 0.1
friction = 0.02
time_step = 0.25


def turn(x, shift, axis):
    return pltpu.roll(x, shift % x.shape[axis], axis)


def euler(h, u, v, depth):
    keep = 1.0 - time_step * friction
    cross = time_step * coriolis
    column = each(lambda a, b: a + b, depth, h)
    flux_x = each(lambda a, b: a * b, column, u)
    flux_y = each(lambda a, b: a * b, column, v)
    next_h = each(lambda a, b, c: a - (b + c), h, along(flux_x), across(flux_y))
    next_u = each(lambda a, b, c: (keep * a + cross * b) - c, u, v, along(h))
    next_v = each(lambda a, b, c: (keep * b - cross * a) - c, u, v, across(h))
    return next_h, next_u, next_v


def each(f, *grids):
    return [[f(*values) for values in zip(*rows)] for rows in zip(*grids)]


def across(x):
    above = [[turn(y, 1, 0) for y in x[-1]]] + x[:-1]
    below = x[1:] + [[turn(y, -1, 0) for y in x[0]]]
    return each(lambda a, b: b - a, above, below)


def along(x):
    return [[b - a for a, b in zip([turn(y[-1], 1, 1)] + y[:-1], y[1:] + [turn(y[0], -1, 1)])] for y in x]


def one_step(state, depth):
    ahead = euler(*euler(*state, depth), depth)
    return [each(lambda a, b: 0.5 * (a + b), x, y) for x, y in zip(state, ahead)]


def swap_groups(x):
    x, width = list(x), LANES // len(x)
    group = lax.broadcasted_iota(jnp.int32, x[0].shape, 1) // width
    bit = 1
    while bit < len(x):
        low = group & bit == 0
        for i in range(len(x)):
            if not i & bit:
                a, b = x[i], x[i + bit]
                x[i] = jnp.where(low, a, turn(b, width * bit, 1))
                x[i + bit] = jnp.where(low, turn(a, -width * bit, 1), b)
        bit *= 2
    return x


def pick(x, index):
    return jnp.take_along_axis(x, index, axis=1)


def interleave(x):
    ways = len(x)
    lane = lax.broadcasted_iota(jnp.int32, x[0].shape, 1)
    width = LANES // ways
    return swap_groups([pick(y, ways * (lane % width) + lane // width) for y in x])


def blocks_of(x):
    return [x[:, LANES * k : LANES * (k + 1)] for k in range(x.shape[1] // LANES)]


def offsets(odd):
    return [pl.multiple_of(HALO * x, HALO) for x in (3 * odd, 1 + odd, 2 - odd, 3 - 3 * odd)]


def edge_kernel(odd, fields, bathymetry, *refs):
    count, parts, rows, width = fields.shape
    outs, (held, held_depth, sems) = refs[: 2 * count], refs[2 * count :]
    copies = [pltpu.make_async_copy(bathymetry, held_depth, sems.at[count])]
    copies += [pltpu.make_async_copy(fields.at[m], held.at[m], sems.at[m]) for m in range(count)]
    for copy in copies:
        copy.start()
    _, outer, inner, _ = offsets(odd[0])
    copies[0].wait()
    depth = []
    for first in (outer, inner):
        depth.append(interleave(blocks_of(scaled_depth(held_depth[pl.ds(first - HALO, HALO)]))))
    for m in range(count):
        copies[1 + m].wait()
        for i, first in enumerate((outer, inner)):
            write_blocks(outs[2 * m + i], parts, depth[(i + m) % 2])
            for f in range(parts):
                unit = HEIGHT_UNIT if f == 0 else SPEED_UNIT
                write_blocks(outs[2 * m + i], f, interleave(blocks_of(unit * held[m, f, pl.ds(first - HALO, HALO)])))


def write_blocks(ref, index, values):
    for k, value in enumerate(values):
        ref[index, :, LANES * k : LANES * (k + 1)] = value


def scaled_depth(hundredths):
    return hundredths.astype(jnp.float32) * (0.01 * HEIGHT_UNIT)


def spread(ref, *index):
    ways = ref.shape[-2] // SUBLANES
    return [ref[(*index, pl.ds(q, SUBLANES, stride=ways), slice(None))] for q in range(ways)]


def unspread(ref, values, *index):
    for q, value in enumerate(values):
        ref[(*index, pl.ds(q, SUBLANES, stride=len(values)), slice(None))] = value


def take_steps(depth, state, steps):
    parts, blocks = state.shape[:2]

    def grid(ref, *index):
        return [list(x) for x in zip(*[spread(ref, *index, k) for k in range(blocks)])]

    def step(i, carry):
        result = one_step([grid(state, f) for f in range(parts)], grid(depth))
        for f in range(parts):
            for k in range(blocks):
                unspread(state, [x[k] for x in result[f]], f, k)
        return carry

    lax.fori_loop(0, steps, step, 0)


def fill(place, blocks, pieces):
    for first, piece in pieces:
        for k in range(blocks):
            place(k, pl.ds(first, piece.shape[0]))[...] = piece[:, LANES * k : LANES * (k + 1)]


def plane(ref, f):
    return lambda k, rows: ref.at[f, k, rows]


def first_round(odd, depth, state, tile, pieces):
    parts, blocks = state.shape[:2]
    places = offsets(odd[0])
    for f in range(parts):
        fill(plane(state, f), blocks, [(first, ref[f]) for first, ref in zip(places, pieces)])
    take_steps(depth, state, STEPS)
    for f in range(parts):
        write_blocks(tile, f, [state[f, k, HALO : 3 * HALO] for k in range(blocks)])


def first_kernel(odd, beyond, own_outer, own_inner, beside, tile, depth, state):
    pieces = beyond, own_outer, own_inner, beside
    places = offsets(odd[0])
    parts, blocks = state.shape[:2]
    fill(lambda k, rows: depth.at[k, rows], blocks, [(first, ref[parts]) for first, ref in zip(places, pieces)])
    first_round(odd, depth, state, tile, pieces)


def second_kernel(odd, depth, beyond, own_outer, own_inner, beside, tile, tall_depth, state):
    parts, blocks = state.shape[:2]
    far = pl.multiple_of(5 * HALO * odd[0], HALO)
    near = pl.multiple_of(5 * HALO * (1 - odd[0]), HALO)
    fill(lambda k, rows: tall_depth.at[k, rows], blocks, [(far, beyond[parts]), (near, beside[parts])])
    tall_depth[:, HALO : 5 * HALO] = depth[...]
    first_round(odd, depth, state, tile, (beyond, own_outer, own_inner, beside))


def second_round(odd, depth, state, beyond, own, beside, steps):
    rows = own.shape[1]
    far = pl.multiple_of(2 * rows * odd[0], rows)
    near = pl.multiple_of(2 * rows * (1 - odd[0]), rows)
    for f in range(own.shape[0]):
        fill(plane(state, f), state.shape[1], [(far, beyond[f]), (rows, own[f]), (near, beside[f])])
    take_steps(depth, state, steps)


def third_kernel(steps, odd, depth, beyond, own, beside, tile, state):
    second_round(odd, depth, state, beyond, own, beside, steps)
    parts, blocks = state.shape[:2]
    for f in range(parts):
        write_blocks(tile, f, [state[f, k, 2 * HALO : 4 * HALO] for k in range(blocks)])


def last_kernel(steps, odd, depth, beyond, own, beside, other, packed, state):
    second_round(odd, depth, state, beyond, own, beside, steps)
    parts, blocks = state.shape[:2]
    ways = packed.shape[0] // blocks
    for f in range(parts):
        for k in range(blocks):
            columns = slice(LANES * k, LANES * (k + 1))
            pieces = []
            for i in range(2):
                pieces.append(other[f, HALO * i : HALO * (i + 1), columns])
                pieces.append(state[f, k, HALO * (i + 2) : HALO * (i + 3)])
            for j, value in enumerate(swap_groups(pieces)):
                packed[ways * k + j, f] = value


def source_kernel(lists, sources):
    members = sources.shape[0]

    def one(member, carry):
        source = member
        for section in range(lists.shape[0] // members - 1, -1, -1):
            source = lists[section * members + source]
        sources[member] = source
        return carry

    lax.fori_loop(0, members, one, 0, unroll=16)


def gather_kernel(stride, sources, before, after):
    pairs, parts = before.shape[:2]
    member = lax.broadcasted_iota(jnp.int32, before.shape[2:], 1) // stride & 1

    def one(pair, carry):
        halves = []
        for half in range(2):
            source = sources[2 * pair + half]
            shift = (stride * (half - (source & 1))) & (LANES - 1)
            halves.append([pltpu.roll(before[source >> 1, f], shift, 1) for f in range(parts)])
        for f in range(parts):
            after[pair, f] = jnp.where(member == 0, halves[0][f], halves[1][f])
        return carry

    lax.fori_loop(0, pairs, one, 0, unroll=8)


def unpack_kernel(arrived, out):
    count, _, rows, width = out.shape
    blocks = width // LANES
    ways = arrived.shape[0] // blocks
    lane = lax.broadcasted_iota(jnp.int32, (HALO, LANES), 1)
    order = LANES // blocks * (lane % blocks) + lane // blocks
    unit = jnp.where(pl.program_id(0) == 0, 1 / HEIGHT_UNIT, 1 / SPEED_UNIT)
    for j in range(ways):
        pieces = swap_groups([arrived[ways * k + j, 0] for k in range(blocks)])
        for i, piece in enumerate(pieces):
            half, m, low = i // 4, i // 2 % 2, i % 2
            k = 2 * j + low
            out[m, 0, HALO * half : HALO * (half + 1), LANES * k : LANES * (k + 1)] = unit * pick(piece, order)


def body(fields, bathymetry, copy_lists):
    count, parts, rows, width = fields.shape
    devices = lax.axis_size("member")
    cycles = copy_lists.shape[0]
    ring = lax.axis_size("row")
    within = [(i, i ^ 1) for i in range(ring)]
    across_chips = [(i, (i + 1 if i % 2 else i - 1) % ring) for i in range(ring)]
    odd = (lax.axis_index("row") % 2).astype(jnp.int32).reshape(1)
    vmem = pl.BlockSpec(memory_space=pltpu.VMEM)
    smem = pl.BlockSpec(memory_space=pltpu.SMEM)
    f32 = functools.partial(jax.ShapeDtypeStruct, dtype=jnp.float32)
    columns = f32((devices, parts, HALO, LANES))

    def call(kernel, out_shape, *args, scratch=(), scalars=1, space=vmem, grant=16 << 20, name=None):
        many = isinstance(out_shape, tuple)
        return pl.pallas_call(
            kernel,
            out_shape=out_shape,
            in_specs=[smem] * scalars + [space] * (len(args) - scalars),
            out_specs=(vmem,) * len(out_shape) if many else vmem,
            scratch_shapes=scratch,
            compiler_params=pltpu.CompilerParams(vmem_limit_bytes=grant),
            name=name,
        )(*args)

    def exchange(outer, inner):
        return lax.ppermute(outer, "row", across_chips), lax.ppermute(inner, "row", within)

    blocks = width // LANES
    half = f32((parts + 1, HALO, width))
    tile = f32((parts, rows, width))
    edges = call(
        edge_kernel,
        (half,) * (2 * count),
        odd,
        pltpu.with_memory_space_constraint(fields, pltpu.HBM),
        pltpu.with_memory_space_constraint(bathymetry, pltpu.HBM),
        scratch=[
            pltpu.VMEM(fields.shape, fields.dtype),
            pltpu.VMEM(bathymetry.shape, bathymetry.dtype),
            pltpu.SemaphoreType.DMA((count + 1,)),
        ],
        space=pl.BlockSpec(memory_space=pltpu.HBM),
        name="edge",
    )
    now = [edges[2 * m : 2 * m + 2] for m in range(count)]
    around = [exchange(*x) for x in now]
    pieces = [(beyond, *x, beside) for x, (beyond, beside) in zip(now, around)]

    sources = pl.pallas_call(
        source_kernel,
        out_shape=jax.ShapeDtypeStruct((count * devices,), jnp.int32),
        in_specs=[smem],
        out_specs=smem,
        compiler_params=pltpu.CompilerParams(vmem_limit_bytes=1 << 20),
        name="sources",
    )(copy_lists.reshape(-1))
    pieces[0], sources = lax.optimization_barrier((pieces[0], sources))

    def state(tall):
        return [pltpu.VMEM((parts, blocks, tall, LANES), jnp.float32)]

    tall = rows + 2 * HALO
    first, depth = call(
        first_kernel, (tile, f32((blocks, tall, LANES))), odd, *pieces[0], scratch=state(tall), name="first"
    )
    around = [exchange(first, first)]
    tall = rows * 3
    second, tall_depth = call(
        second_kernel,
        (tile, f32((blocks, tall, LANES))),
        odd,
        depth,
        *pieces[1],
        scratch=state(rows + 2 * HALO),
        name="second",
    )
    around.append(exchange(second, second))
    steps = (cycles - 1) * STEPS
    first = call(
        functools.partial(third_kernel, steps),
        tile,
        odd,
        tall_depth,
        around[0][0],
        first,
        around[0][1],
        scratch=state(tall),
        name="third",
    )
    packed = call(
        functools.partial(last_kernel, steps),
        columns,
        odd,
        tall_depth,
        around[1][0],
        second,
        around[1][1],
        first,
        scratch=state(tall),
        name="last",
    )

    own = lax.all_to_all(packed, "member", 0, 0, tiled=True)
    chosen = call(
        functools.partial(gather_kernel, width // devices), columns, sources, own, name="gather"
    )
    arrived = lax.all_to_all(chosen, "member", 0, 0, tiled=True)
    return pl.pallas_call(
        unpack_kernel,
        out_shape=f32(fields.shape),
        grid=(parts,),
        in_specs=[pl.BlockSpec((devices, 1, HALO, LANES), lambda f: (0, f, 0, 0))],
        out_specs=pl.BlockSpec((count, 1, rows, width), lambda f: (0, f, 0, 0)),
        compiler_params=pltpu.CompilerParams(vmem_limit_bytes=16 << 20),
        name="unpack",
    )(arrived)


def solution(mesh):
    placed = (P("member", None, "row", None), P("row", None), P())
    return jax.shard_map(
        body, mesh=mesh, in_specs=placed, out_specs=P("member", None, "row", None), check_vma=False
    )
```

```python
import functools

import jax
import jax.numpy as jnp
from jax import lax
from jax.experimental import pallas as pl
from jax.experimental.pallas import tpu as pltpu
from jax.sharding import PartitionSpec as P

STEPS = 4
HALO = 2 * STEPS
LANES = 128
SUBLANES = 8
HEIGHT_UNIT = 2.0**-5
SPEED_UNIT = 2.0**-3

gravity = 2.0
coriolis = 0.1
friction = 0.02
time_step = 0.25


def turn(x, shift, axis):
    return pltpu.roll(x, shift % x.shape[axis], axis)


def euler(h, u, v, depth):
    keep = 1.0 - time_step * friction
    cross = time_step * coriolis
    column = each(lambda a, b: a + b, depth, h)
    flux_x = each(lambda a, b: a * b, column, u)
    flux_y = each(lambda a, b: a * b, column, v)
    next_h = each(lambda a, b, c: a - (b + c), h, along(flux_x), across(flux_y))
    next_u = each(lambda a, b, c: (keep * a + cross * b) - c, u, v, along(h))
    next_v = each(lambda a, b, c: (keep * b - cross * a) - c, u, v, across(h))
    return next_h, next_u, next_v


def each(f, *grids):
    return [[f(*values) for values in zip(*rows)] for rows in zip(*grids)]


def across(x):
    above = [[turn(y, 1, 0) for y in x[-1]]] + x[:-1]
    below = x[1:] + [[turn(y, -1, 0) for y in x[0]]]
    return each(lambda a, b: b - a, above, below)


def along(x):
    return [[b - a for a, b in zip([turn(y[-1], 1, 1)] + y[:-1], y[1:] + [turn(y[0], -1, 1)])] for y in x]


def one_step(state, depth):
    ahead = euler(*euler(*state, depth), depth)
    return [each(lambda a, b: 0.5 * (a + b), x, y) for x, y in zip(state, ahead)]


def swap_groups(x):
    x, width = list(x), LANES // len(x)
    group = lax.broadcasted_iota(jnp.int32, x[0].shape, 1) // width
    bit = 1
    while bit < len(x):
        low = group & bit == 0
        for i in range(len(x)):
            if not i & bit:
                a, b = x[i], x[i + bit]
                x[i] = jnp.where(low, a, turn(b, width * bit, 1))
                x[i + bit] = jnp.where(low, turn(a, -width * bit, 1), b)
        bit *= 2
    return x


def pick(x, index):
    return jnp.take_along_axis(x, index, axis=1)


def interleave(x):
    ways = len(x)
    lane = lax.broadcasted_iota(jnp.int32, x[0].shape, 1)
    width = LANES // ways
    return swap_groups([pick(y, ways * (lane % width) + lane // width) for y in x])


def blocks_of(x):
    return [x[:, LANES * k : LANES * (k + 1)] for k in range(x.shape[1] // LANES)]


def offsets(odd):
    return [pl.multiple_of(HALO * x, HALO) for x in (3 * odd, 1 + odd, 2 - odd, 3 - 3 * odd)]


def edge_kernel(odd, fields, bathymetry, *refs):
    count, parts, rows, width = fields.shape
    outs, (held, held_depth, sems) = refs[: 2 * count], refs[2 * count :]
    copies = [pltpu.make_async_copy(bathymetry, held_depth, sems.at[count])]
    copies += [pltpu.make_async_copy(fields.at[m], held.at[m], sems.at[m]) for m in range(count)]
    for copy in copies:
        copy.start()
    _, outer, inner, _ = offsets(odd[0])
    copies[0].wait()
    depth = []
    for first in (outer, inner):
        depth.append(interleave(blocks_of(scaled_depth(held_depth[pl.ds(first - HALO, HALO)]))))
    for m in range(count):
        copies[1 + m].wait()
        for i, first in enumerate((outer, inner)):
            write_blocks(outs[2 * m + i], parts, depth[(i + m) % 2])
            for f in range(parts):
                unit = HEIGHT_UNIT if f == 0 else SPEED_UNIT
                write_blocks(outs[2 * m + i], f, interleave(blocks_of(unit * held[m, f, pl.ds(first - HALO, HALO)])))


def write_blocks(ref, index, values):
    for k, value in enumerate(values):
        ref[index, :, LANES * k : LANES * (k + 1)] = value


def scaled_depth(hundredths):
    return hundredths.astype(jnp.float32) * (0.01 * HEIGHT_UNIT)


def spread(ref, *index):
    ways = ref.shape[-2] // SUBLANES
    return [ref[(*index, pl.ds(q, SUBLANES, stride=ways), slice(None))] for q in range(ways)]


def unspread(ref, values, *index):
    for q, value in enumerate(values):
        ref[(*index, pl.ds(q, SUBLANES, stride=len(values)), slice(None))] = value


def take_steps(depth, state, steps):
    parts, blocks = state.shape[:2]

    def grid(ref, *index):
        return [list(x) for x in zip(*[spread(ref, *index, k) for k in range(blocks)])]

    def step(i, carry):
        result = one_step([grid(state, f) for f in range(parts)], grid(depth))
        for f in range(parts):
            for k in range(blocks):
                unspread(state, [x[k] for x in result[f]], f, k)
        return carry

    lax.fori_loop(0, steps, step, 0)


def fill(place, blocks, pieces):
    for first, piece in pieces:
        for k in range(blocks):
            place(k, pl.ds(first, piece.shape[0]))[...] = piece[:, LANES * k : LANES * (k + 1)]


def plane(ref, f):
    return lambda k, rows: ref.at[f, k, rows]


def first_round(odd, depth, state, tile, pieces):
    parts, blocks = state.shape[:2]
    places = offsets(odd[0])
    for f in range(parts):
        fill(plane(state, f), blocks, [(first, ref[f]) for first, ref in zip(places, pieces)])
    take_steps(depth, state, STEPS)
    for f in range(parts):
        write_blocks(tile, f, [state[f, k, HALO : 3 * HALO] for k in range(blocks)])


def first_kernel(odd, beyond, own_outer, own_inner, beside, tile, depth, state):
    pieces = beyond, own_outer, own_inner, beside
    places = offsets(odd[0])
    parts, blocks = state.shape[:2]
    fill(lambda k, rows: depth.at[k, rows], blocks, [(first, ref[parts]) for first, ref in zip(places, pieces)])
    first_round(odd, depth, state, tile, pieces)


def second_kernel(odd, depth, beyond, own_outer, own_inner, beside, tile, tall_depth, state):
    parts, blocks = state.shape[:2]
    far = pl.multiple_of(5 * HALO * odd[0], HALO)
    near = pl.multiple_of(5 * HALO * (1 - odd[0]), HALO)
    fill(lambda k, rows: tall_depth.at[k, rows], blocks, [(far, beyond[parts]), (near, beside[parts])])
    tall_depth[:, HALO : 5 * HALO] = depth[...]
    first_round(odd, depth, state, tile, (beyond, own_outer, own_inner, beside))


def second_round(odd, depth, state, beyond, own, beside, steps):
    rows = own.shape[1]
    far = pl.multiple_of(2 * rows * odd[0], rows)
    near = pl.multiple_of(2 * rows * (1 - odd[0]), rows)
    for f in range(own.shape[0]):
        fill(plane(state, f), state.shape[1], [(far, beyond[f]), (rows, own[f]), (near, beside[f])])
    take_steps(depth, state, steps)


def third_kernel(steps, odd, depth, beyond, own, beside, tile, state):
    second_round(odd, depth, state, beyond, own, beside, steps)
    parts, blocks = state.shape[:2]
    for f in range(parts):
        write_blocks(tile, f, [state[f, k, 2 * HALO : 4 * HALO] for k in range(blocks)])


def last_kernel(steps, odd, depth, beyond, own, beside, other, packed, state):
    second_round(odd, depth, state, beyond, own, beside, steps)
    parts, blocks = state.shape[:2]
    ways = packed.shape[0] // blocks
    for f in range(parts):
        for k in range(blocks):
            columns = slice(LANES * k, LANES * (k + 1))
            pieces = []
            for i in range(2):
                pieces.append(other[f, HALO * i : HALO * (i + 1), columns])
                pieces.append(state[f, k, HALO * (i + 2) : HALO * (i + 3)])
            for j, value in enumerate(swap_groups(pieces)):
                packed[ways * k + j, f] = value


def source_kernel(lists, sources):
    members = sources.shape[0]

    def one(member, carry):
        source = member
        for section in range(lists.shape[0] // members - 1, -1, -1):
            source = lists[section * members + source]
        sources[member] = source
        return carry

    lax.fori_loop(0, members, one, 0, unroll=64)


def gather_kernel(stride, sources, before, after):
    pairs, parts = before.shape[:2]
    member = lax.broadcasted_iota(jnp.int32, before.shape[2:], 1) // stride & 1

    def one(pair, carry):
        halves = []
        for half in range(2):
            source = sources[2 * pair + half]
            shift = (stride * (half - (source & 1))) & (LANES - 1)
            halves.append([pltpu.roll(before[source >> 1, f], shift, 1) for f in range(parts)])
        for f in range(parts):
            after[pair, f] = jnp.where(member == 0, halves[0][f], halves[1][f])
        return carry

    lax.fori_loop(0, pairs, one, 0, unroll=8)


def unpack_kernel(arrived, out):
    count, _, rows, width = out.shape
    blocks = width // LANES
    ways = arrived.shape[0] // blocks
    lane = lax.broadcasted_iota(jnp.int32, (HALO, LANES), 1)
    order = LANES // blocks * (lane % blocks) + lane // blocks
    unit = jnp.where(pl.program_id(0) == 0, 1 / HEIGHT_UNIT, 1 / SPEED_UNIT)
    for j in range(ways):
        pieces = swap_groups([arrived[ways * k + j, 0] for k in range(blocks)])
        for i, piece in enumerate(pieces):
            half, m, low = i // 4, i // 2 % 2, i % 2
            k = 2 * j + low
            out[m, 0, HALO * half : HALO * (half + 1), LANES * k : LANES * (k + 1)] = unit * pick(piece, order)


def body(fields, bathymetry, copy_lists):
    count, parts, rows, width = fields.shape
    devices = lax.axis_size("member")
    cycles = copy_lists.shape[0]
    ring = lax.axis_size("row")
    within = [(i, i ^ 1) for i in range(ring)]
    across_chips = [(i, (i + 1 if i % 2 else i - 1) % ring) for i in range(ring)]
    odd = (lax.axis_index("row") % 2).astype(jnp.int32).reshape(1)
    vmem = pl.BlockSpec(memory_space=pltpu.VMEM)
    smem = pl.BlockSpec(memory_space=pltpu.SMEM)
    f32 = functools.partial(jax.ShapeDtypeStruct, dtype=jnp.float32)
    columns = f32((devices, parts, HALO, LANES))

    def call(kernel, out_shape, *args, scratch=(), scalars=1, space=vmem, grant=16 << 20, name=None):
        many = isinstance(out_shape, tuple)
        return pl.pallas_call(
            kernel,
            out_shape=out_shape,
            in_specs=[smem] * scalars + [space] * (len(args) - scalars),
            out_specs=(vmem,) * len(out_shape) if many else vmem,
            scratch_shapes=scratch,
            compiler_params=pltpu.CompilerParams(vmem_limit_bytes=grant),
            name=name,
        )(*args)

    def exchange(outer, inner):
        return lax.ppermute(outer, "row", across_chips), lax.ppermute(inner, "row", within)

    blocks = width // LANES
    half = f32((parts + 1, HALO, width))
    tile = f32((parts, rows, width))
    edges = call(
        edge_kernel,
        (half,) * (2 * count),
        odd,
        pltpu.with_memory_space_constraint(fields, pltpu.HBM),
        pltpu.with_memory_space_constraint(bathymetry, pltpu.HBM),
        scratch=[
            pltpu.VMEM(fields.shape, fields.dtype),
            pltpu.VMEM(bathymetry.shape, bathymetry.dtype),
            pltpu.SemaphoreType.DMA((count + 1,)),
        ],
        space=pl.BlockSpec(memory_space=pltpu.HBM),
        name="edge",
    )
    now = [edges[2 * m : 2 * m + 2] for m in range(count)]
    around = [exchange(*x) for x in now]
    pieces = [(beyond, *x, beside) for x, (beyond, beside) in zip(now, around)]

    sources = pl.pallas_call(
        source_kernel,
        out_shape=jax.ShapeDtypeStruct((count * devices,), jnp.int32),
        in_specs=[smem],
        out_specs=smem,
        compiler_params=pltpu.CompilerParams(vmem_limit_bytes=1 << 20),
        name="sources",
    )(copy_lists.reshape(-1))
    pieces[0], sources = lax.optimization_barrier((pieces[0], sources))

    def state(tall):
        return [pltpu.VMEM((parts, blocks, tall, LANES), jnp.float32)]

    tall = rows + 2 * HALO
    first, depth = call(
        first_kernel, (tile, f32((blocks, tall, LANES))), odd, *pieces[0], scratch=state(tall), name="first"
    )
    around = [exchange(first, first)]
    tall = rows * 3
    second, tall_depth = call(
        second_kernel,
        (tile, f32((blocks, tall, LANES))),
        odd,
        depth,
        *pieces[1],
        scratch=state(rows + 2 * HALO),
        name="second",
    )
    around.append(exchange(second, second))
    steps = (cycles - 1) * STEPS
    first = call(
        functools.partial(third_kernel, steps),
        tile,
        odd,
        tall_depth,
        around[0][0],
        first,
        around[0][1],
        scratch=state(tall),
        name="third",
    )
    packed = call(
        functools.partial(last_kernel, steps),
        columns,
        odd,
        tall_depth,
        around[1][0],
        second,
        around[1][1],
        first,
        scratch=state(tall),
        name="last",
    )

    own = lax.all_to_all(packed, "member", 0, 0, tiled=True)
    chosen = call(
        functools.partial(gather_kernel, width // devices), columns, sources, own, name="gather"
    )
    arrived = lax.all_to_all(chosen, "member", 0, 0, tiled=True)
    return pl.pallas_call(
        unpack_kernel,
        out_shape=f32(fields.shape),
        grid=(parts,),
        in_specs=[pl.BlockSpec((devices, 1, HALO, LANES), lambda f: (0, f, 0, 0))],
        out_specs=pl.BlockSpec((count, 1, rows, width), lambda f: (0, f, 0, 0)),
        compiler_params=pltpu.CompilerParams(vmem_limit_bytes=16 << 20),
        name="unpack",
    )(arrived)


def solution(mesh):
    placed = (P("member", None, "row", None), P("row", None), P())
    return jax.shard_map(
        body, mesh=mesh, in_specs=placed, out_specs=P("member", None, "row", None), check_vma=False
    )
```

```python
import functools

import jax
import jax.numpy as jnp
from jax import lax
from jax.experimental import pallas as pl
from jax.experimental.pallas import tpu as pltpu
from jax.sharding import PartitionSpec as P


STEPS = 4
HALO = 2 * STEPS
LANES = 128
SUBLANES = 8
HEIGHT_UNIT = 2.0**-5
SPEED_UNIT = 2.0**-3

coriolis = 0.1
friction = 0.02
time_step = 0.25


def turn(x, shift, axis):
    return pltpu.roll(x, shift % x.shape[axis], axis)


def euler(h, u, v, depth):
    keep = 1.0 - time_step * friction
    cross = time_step * coriolis
    column = each(lambda a, b: a + b, depth, h)
    flux_x = each(lambda a, b: a * b, column, u)
    flux_y = each(lambda a, b: a * b, column, v)
    next_h = each(lambda a, b, c: a - (b + c), h, along(flux_x), across(flux_y))
    next_u = each(lambda a, b, c: (keep * a + cross * b) - c, u, v, along(h))
    next_v = each(lambda a, b, c: (keep * b - cross * a) - c, u, v, across(h))
    return next_h, next_u, next_v


def each(f, *grids):
    return [[f(*values) for values in zip(*rows)] for rows in zip(*grids)]


def across(x):
    above = [[turn(y, 1, 0) for y in x[-1]]] + x[:-1]
    below = x[1:] + [[turn(y, -1, 0) for y in x[0]]]
    return each(lambda a, b: b - a, above, below)


def along(x):
    return [[b - a for a, b in zip([turn(y[-1], 1, 1)] + y[:-1], y[1:] + [turn(y[0], -1, 1)])] for y in x]


def one_step(state, depth):
    ahead = euler(*euler(*state, depth), depth)
    return [each(lambda a, b: 0.5 * (a + b), x, y) for x, y in zip(state, ahead)]


def swap_groups(x):
    x, width = list(x), LANES // len(x)
    group = lax.broadcasted_iota(jnp.int32, x[0].shape, 1) // width
    bit = 1
    while bit < len(x):
        low = group & bit == 0
        for i in range(len(x)):
            if not i & bit:
                a, b = x[i], x[i + bit]
                x[i] = jnp.where(low, a, turn(b, width * bit, 1))
                x[i + bit] = jnp.where(low, turn(a, -width * bit, 1), b)
        bit *= 2
    return x


def pick(x, index):
    return jnp.take_along_axis(x, index, axis=1)


def interleave(x):
    ways = len(x)
    lane = lax.broadcasted_iota(jnp.int32, x[0].shape, 1)
    width = LANES // ways
    return swap_groups([pick(y, ways * (lane % width) + lane // width) for y in x])


def blocks_of(x):
    return [x[:, LANES * k : LANES * (k + 1)] for k in range(x.shape[1] // LANES)]


def offsets(odd):
    return [pl.multiple_of(HALO * x, HALO) for x in (3 * odd, 1 + odd, 2 - odd, 3 - 3 * odd)]


def edge_kernel(odd, fields, bathymetry, *refs):
    count, parts, _, _ = fields.shape
    outs, (held, held_depth, sems) = refs[: 2 * count], refs[2 * count :]
    copies = [pltpu.make_async_copy(bathymetry, held_depth, sems.at[count])]
    copies += [pltpu.make_async_copy(fields.at[m], held.at[m], sems.at[m]) for m in range(count)]
    for copy in copies:
        copy.start()
    _, outer, inner, _ = offsets(odd[0])
    copies[0].wait()
    depth = []
    for first in (outer, inner):
        depth.append(interleave(blocks_of(scaled_depth(held_depth[pl.ds(first - HALO, HALO)]))))
    for m in range(count):
        copies[1 + m].wait()
        for i, first in enumerate((outer, inner)):
            write_blocks(outs[2 * m + i], parts, depth[(i + m) % 2])
            for f in range(parts):
                unit = HEIGHT_UNIT if f == 0 else SPEED_UNIT
                write_blocks(outs[2 * m + i], f, interleave(blocks_of(unit * held[m, f, pl.ds(first - HALO, HALO)])))


def write_blocks(ref, index, values):
    for k, value in enumerate(values):
        ref[index, :, LANES * k : LANES * (k + 1)] = value


def scaled_depth(hundredths):
    return hundredths.astype(jnp.float32) * (0.01 * HEIGHT_UNIT)


def spread(ref, *index):
    ways = ref.shape[-2] // SUBLANES
    return [ref[(*index, pl.ds(q, SUBLANES, stride=ways), slice(None))] for q in range(ways)]


def unspread(ref, values, *index):
    for q, value in enumerate(values):
        ref[(*index, pl.ds(q, SUBLANES, stride=len(values)), slice(None))] = value


def take_steps(depth, state, steps):
    parts, blocks = state.shape[:2]

    def grid(ref, *index):
        return [list(x) for x in zip(*[spread(ref, *index, k) for k in range(blocks)])]

    def step(i, carry):
        result = one_step([grid(state, f) for f in range(parts)], grid(depth))
        for f in range(parts):
            for k in range(blocks):
                unspread(state, [x[k] for x in result[f]], f, k)
        return carry

    lax.fori_loop(0, steps, step, 0)


def fill(place, blocks, pieces):
    for first, piece in pieces:
        for k in range(blocks):
            place(k, pl.ds(first, piece.shape[0]))[...] = piece[:, LANES * k : LANES * (k + 1)]


def plane(ref, f):
    return lambda k, rows: ref.at[f, k, rows]


def first_round(odd, depth, state, tile, pieces):
    parts, blocks = state.shape[:2]
    places = offsets(odd[0])
    for f in range(parts):
        fill(plane(state, f), blocks, [(first, ref[f]) for first, ref in zip(places, pieces)])
    take_steps(depth, state, STEPS)
    for f in range(parts):
        write_blocks(tile, f, [state[f, k, HALO : 3 * HALO] for k in range(blocks)])


def first_kernel(odd, beyond, own_outer, own_inner, beside, tile, depth, state):
    pieces = beyond, own_outer, own_inner, beside
    places = offsets(odd[0])
    parts, blocks = state.shape[:2]
    fill(lambda k, rows: depth.at[k, rows], blocks, [(first, ref[parts]) for first, ref in zip(places, pieces)])
    first_round(odd, depth, state, tile, pieces)


def second_kernel(odd, depth, beyond, own_outer, own_inner, beside, tile, tall_depth, state):
    parts, blocks = state.shape[:2]
    far = pl.multiple_of(5 * HALO * odd[0], HALO)
    near = pl.multiple_of(5 * HALO * (1 - odd[0]), HALO)
    fill(lambda k, rows: tall_depth.at[k, rows], blocks, [(far, beyond[parts]), (near, beside[parts])])
    tall_depth[:, HALO : 5 * HALO] = depth[...]
    first_round(odd, depth, state, tile, (beyond, own_outer, own_inner, beside))


def second_round(odd, depth, state, beyond, own, beside, steps):
    rows = own.shape[1]
    far = pl.multiple_of(2 * rows * odd[0], rows)
    near = pl.multiple_of(2 * rows * (1 - odd[0]), rows)
    for f in range(own.shape[0]):
        fill(plane(state, f), state.shape[1], [(far, beyond[f]), (rows, own[f]), (near, beside[f])])
    take_steps(depth, state, steps)


def third_kernel(steps, odd, depth, beyond, own, beside, tile, state):
    second_round(odd, depth, state, beyond, own, beside, steps)
    parts, blocks = state.shape[:2]
    for f in range(parts):
        write_blocks(tile, f, [state[f, k, 2 * HALO : 4 * HALO] for k in range(blocks)])


def last_kernel(steps, odd, depth, beyond, own, beside, other, packed, state):
    second_round(odd, depth, state, beyond, own, beside, steps)
    parts, blocks = state.shape[:2]
    ways = packed.shape[0] // blocks
    for f in range(parts):
        for k in range(blocks):
            columns = slice(LANES * k, LANES * (k + 1))
            pieces = []
            for i in range(2):
                pieces.append(other[f, HALO * i : HALO * (i + 1), columns])
                pieces.append(state[f, k, HALO * (i + 2) : HALO * (i + 3)])
            for j, value in enumerate(swap_groups(pieces)):
                packed[ways * k + j, f] = value


def source_kernel(lists, sources):
    members = sources.shape[0]

    def one(member, carry):
        source = member
        for section in range(lists.shape[0] // members - 1, -1, -1):
            source = lists[section * members + source]
        sources[member] = source
        return carry

    lax.fori_loop(0, members, one, 0, unroll=16)


def gather_kernel(stride, sources, before, after):
    pairs, parts = before.shape[:2]
    member = lax.broadcasted_iota(jnp.int32, before.shape[2:], 1) // stride & 1

    def one(pair, carry):
        halves = []
        for half in range(2):
            source = sources[2 * pair + half]
            shift = (stride * (half - (source & 1))) & (LANES - 1)
            halves.append([pltpu.roll(before[source >> 1, f], shift, 1) for f in range(parts)])
        for f in range(parts):
            after[pair, f] = jnp.where(member == 0, halves[0][f], halves[1][f])
        return carry

    lax.fori_loop(0, pairs, one, 0, unroll=8)


def unpack_kernel(arrived, out):
    _, _, _, width = out.shape
    blocks = width // LANES
    ways = arrived.shape[0] // blocks
    lane = lax.broadcasted_iota(jnp.int32, (HALO, LANES), 1)
    order = LANES // blocks * (lane % blocks) + lane // blocks
    unit = jnp.where(pl.program_id(0) == 0, 1 / HEIGHT_UNIT, 1 / SPEED_UNIT)
    for j in range(ways):
        pieces = swap_groups([arrived[ways * k + j, 0] for k in range(blocks)])
        for i, piece in enumerate(pieces):
            half, m, low = i // 4, i // 2 % 2, i % 2
            k = 2 * j + low
            out[m, 0, HALO * half : HALO * (half + 1), LANES * k : LANES * (k + 1)] = unit * pick(piece, order)


def body(fields, bathymetry, copy_lists):
    count, parts, rows, width = fields.shape
    devices = lax.axis_size("member")
    cycles = copy_lists.shape[0]
    ring = lax.axis_size("row")
    within = [(i, i ^ 1) for i in range(ring)]
    across_chips = [(i, (i + 1 if i % 2 else i - 1) % ring) for i in range(ring)]
    odd = (lax.axis_index("row") % 2).astype(jnp.int32).reshape(1)
    vmem = pl.BlockSpec(memory_space=pltpu.VMEM)
    smem = pl.BlockSpec(memory_space=pltpu.SMEM)
    f32 = functools.partial(jax.ShapeDtypeStruct, dtype=jnp.float32)
    columns = f32((devices, parts, HALO, LANES))

    def call(kernel, out_shape, *args, scratch=(), scalars=1, space=vmem, grant=16 << 20):
        many = isinstance(out_shape, tuple)
        return pl.pallas_call(
            kernel,
            out_shape=out_shape,
            in_specs=[smem] * scalars + [space] * (len(args) - scalars),
            out_specs=(vmem,) * len(out_shape) if many else vmem,
            scratch_shapes=scratch,
            compiler_params=pltpu.CompilerParams(vmem_limit_bytes=grant),
        )(*args)

    def exchange(outer, inner):
        return lax.ppermute(outer, "row", across_chips), lax.ppermute(inner, "row", within)

    blocks = width // LANES
    half = f32((parts + 1, HALO, width))
    tile = f32((parts, rows, width))
    edges = call(
        edge_kernel,
        (half,) * (2 * count),
        odd,
        pltpu.with_memory_space_constraint(fields, pltpu.HBM),
        pltpu.with_memory_space_constraint(bathymetry, pltpu.HBM),
        scratch=[
            pltpu.VMEM(fields.shape, fields.dtype),
            pltpu.VMEM(bathymetry.shape, bathymetry.dtype),
            pltpu.SemaphoreType.DMA((count + 1,)),
        ],
        space=pl.BlockSpec(memory_space=pltpu.HBM),
    )
    now = [edges[2 * m : 2 * m + 2] for m in range(count)]
    around = [exchange(*x) for x in now]
    pieces = [(beyond, *x, beside) for x, (beyond, beside) in zip(now, around)]

    sources = pl.pallas_call(
        source_kernel,
        out_shape=jax.ShapeDtypeStruct((count * devices,), jnp.int32),
        in_specs=[smem],
        out_specs=smem,
        compiler_params=pltpu.CompilerParams(vmem_limit_bytes=1 << 20),
        name="sources",
    )(copy_lists.reshape(-1))

    def state(tall):
        return [pltpu.VMEM((parts, blocks, tall, LANES), jnp.float32)]

    tall = rows + 2 * HALO
    first, depth = call(first_kernel, (tile, f32((blocks, tall, LANES))), odd, *pieces[0], scratch=state(tall))
    around = [exchange(first, first)]
    tall = rows * 3
    second, tall_depth = call(
        second_kernel, (tile, f32((blocks, tall, LANES))), odd, depth, *pieces[1], scratch=state(rows + 2 * HALO)
    )
    beyond = lax.ppermute(second, "row", across_chips)
    around.append((beyond, lax.ppermute(second, "row", within)))
    steps = (cycles - 1) * STEPS
    first = call(
        functools.partial(third_kernel, steps),
        tile,
        odd,
        tall_depth,
        around[0][0],
        first,
        around[0][1],
        scratch=state(tall),
    )
    packed = call(
        functools.partial(last_kernel, steps),
        columns,
        odd,
        tall_depth,
        around[1][0],
        second,
        around[1][1],
        first,
        scratch=state(tall),
    )

    own = lax.all_to_all(packed, "member", 0, 0, tiled=True)
    chosen = call(functools.partial(gather_kernel, width // devices), columns, sources, own)
    arrived = lax.all_to_all(chosen, "member", 0, 0, tiled=True)
    return pl.pallas_call(
        unpack_kernel,
        out_shape=f32(fields.shape),
        grid=(parts,),
        in_specs=[pl.BlockSpec((devices, 1, HALO, LANES), lambda f: (0, f, 0, 0))],
        out_specs=pl.BlockSpec((count, 1, rows, width), lambda f: (0, f, 0, 0)),
        compiler_params=pltpu.CompilerParams(vmem_limit_bytes=16 << 20),
        name="unpack",
    )(arrived)


def solution(mesh):
    placed = (P("member", None, "row", None), P("row", None), P())
    return jax.shard_map(body, mesh=mesh, in_specs=placed, out_specs=P("member", None, "row", None), check_vma=False)
```
